512 devices in a mesh: row: 16 (over y, core), col: 32 (over x, z).
Axes of the slice: x: 4, y: 8, z: 8, core: 2. Of those that a mesh axis runs over, the one named last changes fastest.
Arguments:
- a_blocks: bfloat16 [32768, 4096], P(('row', 'col')), may hold values from -0.75 to 0.75
- blk_row: int32 [32768], P(('row', 'col')), may hold values from 0 to 4095, as said below
- blk_col: int32 [32768], P(('row', 'col')), may hold values from 0 to 4095, as said below
- drop_mask: int32 [32768], P(('row', 'col')), may hold values 0 or 1
- prolong: bfloat16 [4096, 1024], P(('row', 'col')), may hold values from -6 to 6
- agg_label: int32 [4096], P(('row', 'col')), may hold values from 0 to 1
- inv_diag: bfloat16 [4096, 4096], P(('row', 'col'))
Outputs:
- coarse: float32 [32768, 1024], P(('row', 'col'))
The draws below stay inside these ranges and needn't reach their ends.
Inputs may be any that keep to these rules, and one draw needn't show every extreme that they name: `blk_row`: blocks stand 64 to a device, devices in row-major order over (row, col); a block on the device (r, c) has its row element in r * 256 to (r + 1) * 256 - 1. Every element is the row and column of one block. `blk_col`: A block on the device (r, c) has a column element e with (e // 8) % (size of col) = c.
All inputs are finite; a program needn't handle non-finite values. No bound on the sum of `drop_mask` on one device may be relied on, other than what follows from the above.
Results may differ from the reference program's by a relative error of at most 0.0003.
Values may be sent and summed in bfloat16 or wider, within the bound.
No kernel may reach another device: no remote copies, remote signals or barrier semaphores. Data moves between devices by JAX's collectives and lax.ppermute only.
A program may use at most 64 MiB of HBM per device.

```python
import jax
import jax.numpy as jnp
from jax import lax

BS = 64
PC = 16
LABELS = 2
ELD = 8
SLOT = 64
ELEMS = 4096
BLOCKS = 32768
N_ROW = 16
N_COL = 32
DEVICES = 512


def build_blocks(key):
    row_span = N_COL * ELD
    device_count = N_ROW * N_COL
    devices = jnp.arange(device_count, dtype=jnp.int32)
    local_ids = jnp.arange(ELD, dtype=jnp.int32)
    diagonal = devices[:, None] * ELD + local_ids[None, :]
    near_slot = jnp.arange(3 * ELD, dtype=jnp.int32) // 3
    near_row = devices[:, None] * ELD + near_slot[None, :]
    offsets = jax.random.randint(jax.random.fold_in(key, 11), (device_count, 3 * ELD), 1, max(ELD, 2))
    near_col = devices[:, None] * ELD + (near_slot[None, :] + offsets) % ELD

    def panel_order(panel):
        return jax.random.permutation(jax.random.fold_in(jax.random.fold_in(key, 12), panel), 4 * row_span).astype(jnp.int32)
    orders = jax.vmap(panel_order)(jnp.arange(N_ROW, dtype=jnp.int32))
    far_row = (jnp.arange(N_ROW, dtype=jnp.int32)[:, None] * row_span + orders // 4).reshape(device_count, 4 * ELD)
    places = jax.random.randint(jax.random.fold_in(key, 13), (device_count, 4 * ELD), 0, N_ROW * ELD)
    col_of_device = devices % N_COL
    far_col = (places // ELD * N_COL + col_of_device[:, None]) * ELD + places % ELD
    rows = jnp.concatenate([diagonal, near_row, far_row], axis=1).reshape(-1)
    cols = jnp.concatenate([diagonal, near_col, far_col], axis=1).reshape(-1)
    return (rows.astype(jnp.int32), cols.astype(jnp.int32))


def draw_blk_row(key, part):
    return build_blocks(key)[0]


def draw_blk_col(key, part):
    return build_blocks(key)[1]


def draw_inv_diag(key, part):
    first_key, second_key = jax.random.split(key)
    lower, upper, spread = (0.5, 2.0, 0.1)
    diag_values = jax.random.uniform(first_key, (ELEMS, BS), jnp.float32, lower, upper)
    off_values = jax.random.normal(second_key, (ELEMS, BS, BS), jnp.float32) * spread
    identity = jnp.eye(BS, dtype=jnp.float32)
    matrices = off_values * (1.0 - identity) + identity * diag_values[:, :, None]
    return matrices.reshape(ELEMS, BS * BS).astype(jnp.bfloat16)


def with_ends(entries, own_key, low, largest):
    dims = entries.shape
    index_at = [jax.random.randint(jax.random.fold_in(own_key, axis), (), 0, dims[axis]) for axis in range(len(dims))]
    entries = entries.at[tuple(index_at)].set(low)
    longest = dims.index(max(dims))
    index_at[longest] = (index_at[longest] + 1) % dims[longest]
    return entries.at[tuple(index_at)].set(largest)


def block_scale(own_key, extent, cuts, low, top_value):
    gain = 1.0
    for position, parts in cuts:
        heights = jax.random.uniform(jax.random.fold_in(jax.random.fold_in(own_key, 6), position), (parts,), jnp.float32, low / len(cuts), top_value / len(cuts))
        gain = gain * jnp.repeat(jnp.exp(heights), extent[position] // parts).reshape((-1,) + (1,) * (len(extent) - 1 - position))
    return gain


def centred(key, extent, deviation, reach, cuts=(), kind=jnp.bfloat16):
    loudness = block_scale(key, extent, cuts, -0.22, 0.18) if cuts else 1.0
    values = jax.random.normal(key, extent, jnp.float32) * deviation * loudness
    return jnp.minimum(jnp.maximum(values, -reach), reach).astype(kind)


def setup_inputs(seed: int = 0) -> dict:
    arg_keys = jax.random.split(jax.random.key(seed), 8)
    a_blocks = centred(arg_keys[0], (BLOCKS, BS * BS), BS ** -0.5, 0.75, ((0, 512),))
    blk_row = draw_blk_row(jax.random.fold_in(arg_keys[7], 71), 0)
    blk_col = draw_blk_col(jax.random.fold_in(arg_keys[7], 71), 0)
    drop_mask = with_ends((jax.random.randint(arg_keys[3], (BLOCKS,), 0, 3) < 2).astype(jnp.int32), jax.random.fold_in(arg_keys[3], 1), 0, 1)
    prolong = centred(arg_keys[4], (ELEMS, BS * PC), 1.0, 6.0, ((0, 512),))
    agg_label = with_ends(jax.random.randint(arg_keys[5], (ELEMS,), 0, LABELS), jax.random.fold_in(arg_keys[5], 1), 0, LABELS - 1).astype(jnp.int32)
    inv_diag = draw_inv_diag(jax.random.fold_in(arg_keys[7], 71), 0)
    return dict(a_blocks=a_blocks, blk_row=blk_row, blk_col=blk_col, drop_mask=drop_mask, prolong=prolong, agg_label=agg_label, inv_diag=inv_diag)


def reference(a_blocks, blk_row, blk_col, drop_mask, prolong, agg_label, inv_diag):
    highest = lax.Precision.HIGHEST
    keep = jnp.maximum(drop_mask, (blk_row == blk_col).astype(jnp.int32))

    def device_terms(items):
        blocks, rows, cols, keeps = items
        matrices = blocks.astype(jnp.float32).reshape(-1, BS, BS)
        col_part = prolong[cols].astype(jnp.float32).reshape(-1, BS, PC)
        row_part = prolong[rows].astype(jnp.float32).reshape(-1, BS, PC)
        keep_float = keeps.astype(jnp.float32)[:, None, None]
        kept_terms = jnp.einsum("sij,sjk->sik", matrices, col_part, precision=highest) * keep_float
        drop_terms = jnp.einsum("sij,sjk->sik", matrices, row_part, precision=highest) * (1.0 - keep_float)
        return kept_terms.reshape(-1, BS * PC), drop_terms.reshape(-1, BS * PC)

    kept_all, drop_all = lax.map(device_terms, (a_blocks.reshape(DEVICES, SLOT, BS * BS), blk_row.reshape(DEVICES, SLOT), blk_col.reshape(DEVICES, SLOT), keep.reshape(DEVICES, SLOT)))
    lumped = jax.ops.segment_sum(drop_all.reshape(BLOCKS, BS * PC), blk_row, num_segments=ELEMS)

    def device_out(items):
        kept_terms, rows, cols = items
        col_run = cols // ELD
        row_run = rows // ELD
        col_label = agg_label[cols]
        same_group = (rows[:, None] == rows[None, :]) & (col_run[:, None] == col_run[None, :]) & (col_label[:, None] == col_label[None, :])
        grouped = jnp.dot(same_group.astype(jnp.float32), kept_terms, precision=highest)
        target = ((col_run == row_run) & (col_label == agg_label[rows])).astype(jnp.float32)
        grouped = grouped + target[:, None] * lumped[rows]
        inverse = inv_diag[rows].astype(jnp.float32).reshape(-1, BS, BS)
        coarse = jnp.einsum("sij,sjk->sik", inverse, grouped.reshape(-1, BS, PC), precision=highest)
        return coarse.reshape(-1, BS * PC)

    coarse = lax.map(device_out, (kept_all, blk_row.reshape(DEVICES, SLOT), blk_col.reshape(DEVICES, SLOT)))
    return coarse.reshape(BLOCKS, BS * PC)
```

```python
import jax
import jax.numpy as jnp
from jax import lax
from jax.sharding import PartitionSpec as P

BS = 64
PC = 16
NX = 4
NZ = 8
HIGHEST = lax.Precision.HIGHEST
F32 = jnp.float32
BF16 = jnp.bfloat16

X_GROUPS = [[x * NZ + z for x in range(NX)] for z in range(NZ)]
Z_GROUPS = [[x * NZ + z for z in range(NZ)] for x in range(NX)]


def shift_x(step):
    return [(x * NZ + z, (x + step) % NX * NZ + z) for x in range(NX) for z in range(NZ)]


def spread(values, groups):
    count = len(groups[0])
    copies = jnp.broadcast_to(values[None], (count,) + values.shape)
    return lax.all_to_all(copies, "col", 0, 0, axis_index_groups=groups, tiled=True)


def body(a_blocks, blk_row, blk_col, drop_mask, prolong, agg_label, inv_diag):
    slot_count = a_blocks.shape[0]
    per_device = prolong.shape[0]
    width = prolong.shape[1]
    col_count = lax.axis_size("col")
    row_index = lax.axis_index("row")
    col_index = lax.axis_index("col")
    span = col_count * per_device
    panel_first = row_index * span
    own_first = panel_first + col_index * per_device

    both = spread(jnp.concatenate([prolong, inv_diag], axis=1), Z_GROUPS)
    both = both.reshape(NZ * per_device, width + inv_diag.shape[1])
    row_part = both[:, :width]
    inv_part = both[:, width:]
    inv_parts = [inv_part] + [lax.ppermute(inv_part, "col", shift_x(k)) for k in (1, 2, 3)]
    row_panel = spread(row_part, X_GROUPS).reshape(span, width)

    labelled = jnp.concatenate(
        [prolong, jnp.broadcast_to(agg_label.astype(BF16)[:, None], (per_device, 128))], axis=1
    )
    col_panel = lax.all_gather(labelled, "row", axis=0, tiled=True)

    keep = (drop_mask == 1) | (blk_row == blk_col)
    local_row = blk_row - panel_first
    matrices = a_blocks.reshape(slot_count, BS, BS)

    pick = (local_row[:, None] == jnp.arange(span)[None, :]) & ~keep[:, None]
    row_blocks = jnp.dot(pick.astype(BF16), row_panel, preferred_element_type=F32).astype(BF16)
    drop_terms = jnp.einsum(
        "sij,sjk->sik", matrices, row_blocks.reshape(slot_count, BS, PC), preferred_element_type=F32
    ).reshape(slot_count, width)
    place = (jnp.arange(span)[:, None] == local_row[None, :]).astype(F32)
    sums = jnp.dot(place, drop_terms, precision=HIGHEST).reshape(col_count, per_device, width)
    arrived = lax.all_to_all(sums, "col", 0, 0, tiled=True)
    lumped = jnp.sum(arrived.reshape(col_count, per_device, width), axis=0)
    scaled_lumped = jnp.einsum(
        "eij,ejk->eik",
        inv_diag.astype(F32).reshape(per_device, BS, BS),
        lumped.reshape(per_device, BS, PC),
        precision=HIGHEST,
    ).reshape(per_device, width)

    col_place = blk_col // span * per_device + blk_col % per_device
    pick = col_place[:, None] == jnp.arange(col_panel.shape[0])[None, :]
    picked = jnp.dot(pick.astype(BF16), col_panel, preferred_element_type=F32)
    col_label = picked[:, width]
    col_blocks = (picked[:, :width] * keep[:, None].astype(F32)).astype(BF16)
    kept_terms = jnp.einsum(
        "sij,sjk->sik", matrices, col_blocks.reshape(slot_count, BS, PC), preferred_element_type=F32
    ).reshape(slot_count, width)
    col_run = blk_col // per_device
    row_run = blk_row // per_device
    same_group = (
        (blk_row[:, None] == blk_row[None, :])
        & (col_run[:, None] == col_run[None, :])
        & (col_label[:, None] == col_label[None, :])
    )
    grouped = jnp.dot(same_group.astype(F32), kept_terms, precision=HIGHEST)

    col_x = col_index // NZ
    part_rows = NZ * per_device
    row_x = local_row // part_rows
    inverse = None
    for step, part in enumerate(inv_parts):
        at = jnp.where((col_x - row_x) % NX == step, local_row % part_rows, -1)
        pick = (at[:, None] == jnp.arange(part_rows)[None, :]).astype(BF16)
        piece = jnp.dot(pick, part, preferred_element_type=F32)
        inverse = piece if inverse is None else inverse + piece
    coarse = jnp.einsum(
        "sij,sjk->sik",
        inverse.reshape(slot_count, BS, BS),
        grouped.reshape(slot_count, BS, PC),
        precision=HIGHEST,
    ).reshape(slot_count, width)

    target = (
        (blk_row[:, None] == own_first + jnp.arange(per_device)[None, :])
        & (col_run == row_run)[:, None]
        & (col_label[:, None] == agg_label.astype(F32)[None, :])
    )
    return coarse + jnp.dot(target.astype(F32), scaled_lumped, precision=HIGHEST)


def solution(mesh):
    return jax.shard_map(
        body,
        mesh=mesh,
        in_specs=(
            P(("row", "col"), None),
            P(("row", "col")),
            P(("row", "col")),
            P(("row", "col")),
            P(("row", "col"), None),
            P(("row", "col")),
            P(("row", "col"), None),
        ),
        out_specs=P(("row", "col"), None),
        check_vma=False,
    )
```

```python
import jax
import jax.numpy as jnp
from jax import lax
from jax.sharding import PartitionSpec as P

BS = 64
PC = 16
NX = 4
NZ = 8
HIGHEST = lax.Precision.HIGHEST
F32 = jnp.float32
BF16 = jnp.bfloat16

X_GROUPS = [[x * NZ + z for x in range(NX)] for z in range(NZ)]
Z_GROUPS = [[x * NZ + z for z in range(NZ)] for x in range(NX)]


def shift_x(step):
    return [(x * NZ + z, (x + step) % NX * NZ + z) for x in range(NX) for z in range(NZ)]


def spread(values, groups):
    count = len(groups[0])
    copies = jnp.broadcast_to(values[None], (count,) + values.shape)
    return lax.all_to_all(copies, "col", 0, 0, axis_index_groups=groups, tiled=True)


def two_parts(values):
    high = lax.reduce_precision(values, 8, 7)
    return high.astype(BF16), (values - high).astype(BF16)


def body(a_blocks, blk_row, blk_col, drop_mask, prolong, agg_label, inv_diag):
    slot_count = a_blocks.shape[0]
    per_device = prolong.shape[0]
    width = prolong.shape[1]
    col_count = lax.axis_size("col")
    row_index = lax.axis_index("row")
    col_index = lax.axis_index("col")
    span = col_count * per_device
    panel_first = row_index * span
    own_first = panel_first + col_index * per_device

    both = spread(jnp.concatenate([prolong, inv_diag], axis=1), Z_GROUPS)
    both = both.reshape(NZ * per_device, width + inv_diag.shape[1])
    row_part = both[:, :width]
    inv_part = both[:, width:]
    row_panel = spread(row_part, X_GROUPS).reshape(span, width)
    inv_parts = [inv_part]
    for k in (1, 2, 3):
        inv_parts.append(lax.ppermute(inv_part, "col", shift_x(k)))

    labelled = jnp.concatenate(
        [prolong, jnp.broadcast_to(agg_label.astype(BF16)[:, None], (per_device, 128))], axis=1
    )
    col_panel = lax.all_gather(labelled, "row", axis=0, tiled=True)

    keep = (drop_mask == 1) | (blk_row == blk_col)
    local_row = blk_row - panel_first
    matrices = a_blocks.reshape(slot_count, BS, BS)

    pick = (local_row[:, None] == jnp.arange(span)[None, :]) & ~keep[:, None]
    row_blocks = jnp.dot(pick.astype(BF16), row_panel, preferred_element_type=F32).astype(BF16)
    drop_terms = jnp.einsum(
        "sij,sjk->sik", matrices, row_blocks.reshape(slot_count, BS, PC), preferred_element_type=F32
    ).reshape(slot_count, width)
    place = (jnp.arange(span)[:, None] == local_row[None, :]).astype(BF16)
    parts = jnp.concatenate(two_parts(drop_terms), axis=0)
    sums = jnp.dot(jnp.concatenate([place, place], axis=1), parts, preferred_element_type=F32)
    sums = sums.reshape(col_count, per_device, width)
    arrived = lax.all_to_all(sums, "col", 0, 0, tiled=True)
    lumped = jnp.sum(arrived.reshape(col_count, per_device, width), axis=0)
    scaled_lumped = jnp.einsum(
        "eij,ejk->eik",
        inv_diag.astype(F32).reshape(per_device, BS, BS),
        lumped.reshape(per_device, BS, PC),
        precision=HIGHEST,
    ).reshape(per_device, width)

    col_place = blk_col // span * per_device + blk_col % per_device
    pick = col_place[:, None] == jnp.arange(col_panel.shape[0])[None, :]
    picked = jnp.dot(pick.astype(BF16), col_panel, preferred_element_type=F32)
    col_label = picked[:, width]
    col_blocks = (picked[:, :width] * keep[:, None].astype(F32)).astype(BF16)
    kept_terms = jnp.einsum(
        "sij,sjk->sik", matrices, col_blocks.reshape(slot_count, BS, PC), preferred_element_type=F32
    ).reshape(slot_count, width)
    col_run = blk_col // per_device
    row_run = blk_row // per_device
    same_group = (
        (blk_row[:, None] == blk_row[None, :])
        & (col_run[:, None] == col_run[None, :])
        & (col_label[:, None] == col_label[None, :])
    )
    same_group = same_group.astype(BF16)
    parts = jnp.concatenate(two_parts(kept_terms), axis=0)
    grouped = jnp.dot(
        jnp.concatenate([same_group, same_group], axis=1), parts, preferred_element_type=F32
    )

    col_x = col_index // NZ
    part_rows = NZ * per_device
    row_x = local_row // part_rows
    inverse = None
    for step, part in enumerate(inv_parts):
        at = jnp.where((col_x - row_x) % NX == step, local_row % part_rows, -1)
        pick = (at[:, None] == jnp.arange(part_rows)[None, :]).astype(BF16)
        piece = jnp.dot(pick, part, preferred_element_type=F32)
        inverse = piece if inverse is None else inverse + piece
    inverse = inverse.astype(BF16).reshape(slot_count, BS, BS)
    parts = [part.reshape(slot_count, BS, PC) for part in two_parts(grouped)]
    coarse = jnp.einsum(
        "sij,sjk->sik", inverse, jnp.concatenate(parts, axis=2), preferred_element_type=F32
    )
    coarse = (coarse[:, :, :PC] + coarse[:, :, PC:]).reshape(slot_count, width)

    target = (
        (blk_row[:, None] == own_first + jnp.arange(per_device)[None, :])
        & (col_run == row_run)[:, None]
        & (col_label[:, None] == agg_label.astype(F32)[None, :])
    )
    return coarse + jnp.dot(target.astype(F32), scaled_lumped, precision=HIGHEST)


def solution(mesh):
    return jax.shard_map(
        body,
        mesh=mesh,
        in_specs=(
            P(("row", "col"), None),
            P(("row", "col")),
            P(("row", "col")),
            P(("row", "col")),
            P(("row", "col"), None),
            P(("row", "col")),
            P(("row", "col"), None),
        ),
        out_specs=P(("row", "col"), None),
        check_vma=False,
    )
```

```python
import jax
import jax.numpy as jnp
from jax import lax
from jax.sharding import PartitionSpec as P

BS = 64
PC = 16
NX = 4
NZ = 8
HIGHEST = lax.Precision.HIGHEST
F32 = jnp.float32
BF16 = jnp.bfloat16

X_GROUPS = [[x * NZ + z for x in range(NX)] for z in range(NZ)]
Z_GROUPS = [[x * NZ + z for z in range(NZ)] for x in range(NX)]


def spread(values, groups):
    count = len(groups[0])
    copies = jnp.broadcast_to(values[None], (count,) + values.shape)
    moved = lax.all_to_all(copies, "col", 0, 0, axis_index_groups=groups, tiled=True)
    return moved.reshape((count * values.shape[0],) + values.shape[1:])


def shift_x(step):
    return [(x * NZ + z, (x + step) % NX * NZ + z) for x in range(NX) for z in range(NZ)]


def two_parts(values):
    high = lax.reduce_precision(values, 8, 7)
    return high.astype(BF16), (values - high).astype(BF16)


def body(a_blocks, blk_row, blk_col, drop_mask, prolong, agg_label, inv_diag):
    slot_count = a_blocks.shape[0]
    per_device = prolong.shape[0]
    width = prolong.shape[1]
    col_count = lax.axis_size("col")
    row_index = lax.axis_index("row")
    col_index = lax.axis_index("col")
    span = col_count * per_device
    panel_first = row_index * span
    own_first = panel_first + col_index * per_device

    both = jnp.concatenate([prolong, inv_diag], axis=1)
    both = spread(both, Z_GROUPS)
    row_panel = spread(both[:, :width], X_GROUPS)
    inv_parts = [both[:, width:]]
    for k in (1, 2, 3):
        inv_parts.append(lax.ppermute(inv_parts[0], "col", shift_x(k)))

    labelled = jnp.concatenate(
        [prolong, jnp.broadcast_to(agg_label.astype(BF16)[:, None], (per_device, 128))], axis=1
    )
    col_panel = lax.all_gather(labelled, "row", axis=0, tiled=True)

    keep = (drop_mask == 1) | (blk_row == blk_col)
    local_row = blk_row - panel_first
    matrices = a_blocks.reshape(slot_count, BS, BS)

    pick = (local_row[:, None] == jnp.arange(span)[None, :]) & ~keep[:, None]
    row_blocks = jnp.dot(pick.astype(BF16), row_panel, preferred_element_type=F32).astype(BF16)
    drop_terms = jnp.einsum(
        "sij,sjk->sik",
        matrices,
        row_blocks.reshape(slot_count, BS, PC),
        preferred_element_type=F32,
    ).reshape(slot_count, width)
    place = (jnp.arange(span)[:, None] == local_row[None, :]).astype(BF16)
    parts = jnp.concatenate(two_parts(drop_terms), axis=0)
    sums = jnp.dot(jnp.concatenate([place, place], axis=1), parts, preferred_element_type=F32)
    sums = sums.reshape(col_count, per_device, width)
    arrived = lax.all_to_all(sums, "col", 0, 0, tiled=True)
    lumped = jnp.sum(arrived.reshape(col_count, per_device, width), axis=0)
    scaled_lumped = jnp.einsum(
        "eij,ejk->eik",
        inv_diag.astype(F32).reshape(per_device, BS, BS),
        lumped.reshape(per_device, BS, PC),
        precision=HIGHEST,
    ).reshape(per_device, width)

    col_place = blk_col // span * per_device + blk_col % per_device
    pick = col_place[:, None] == jnp.arange(col_panel.shape[0])[None, :]
    picked = jnp.dot(pick.astype(BF16), col_panel, preferred_element_type=F32)
    col_label = picked[:, width]
    col_blocks = (picked[:, :width] * keep[:, None].astype(F32)).astype(BF16)
    kept_terms = jnp.einsum(
        "sij,sjk->sik",
        matrices,
        col_blocks.reshape(slot_count, BS, PC),
        preferred_element_type=F32,
    ).reshape(slot_count, width)
    col_run = blk_col // per_device
    row_run = blk_row // per_device
    same_group = (
        (blk_row[:, None] == blk_row[None, :])
        & (col_run[:, None] == col_run[None, :])
        & (col_label[:, None] == col_label[None, :])
    ).astype(BF16)
    parts = jnp.concatenate(two_parts(kept_terms), axis=0)
    grouped = jnp.dot(
        jnp.concatenate([same_group, same_group], axis=1), parts, preferred_element_type=F32
    )

    part_rows = NZ * per_device
    row_x = local_row // part_rows
    inverse = None
    for k in (0, 1, 3, 2):
        at = jnp.where((col_index // NZ - row_x) % NX == k, local_row % part_rows, -1)
        pick = (at[:, None] == jnp.arange(part_rows)[None, :]).astype(BF16)
        piece = jnp.dot(pick, inv_parts[k], preferred_element_type=F32)
        inverse = piece if inverse is None else inverse + piece
    inverse = inverse.astype(BF16)
    inverse = inverse.reshape(slot_count, BS, BS)
    parts = [part.reshape(slot_count, BS, PC) for part in two_parts(grouped)]
    coarse = jnp.einsum(
        "sij,sjk->sik", inverse, jnp.concatenate(parts, axis=2), preferred_element_type=F32
    )
    coarse = (coarse[:, :, :PC] + coarse[:, :, PC:]).reshape(slot_count, width)

    target = (
        (blk_row[:, None] == own_first + jnp.arange(per_device)[None, :])
        & (col_run == row_run)[:, None]
        & (col_label[:, None] == agg_label.astype(F32)[None, :])
    )
    return coarse + jnp.dot(target.astype(F32), scaled_lumped, precision=HIGHEST)


def solution(mesh):
    return jax.shard_map(
        body,
        mesh=mesh,
        in_specs=(
            P(("row", "col"), None),
            P(("row", "col")),
            P(("row", "col")),
            P(("row", "col")),
            P(("row", "col"), None),
            P(("row", "col")),
            P(("row", "col"), None),
        ),
        out_specs=P(("row", "col"), None),
        check_vma=False,
    )
```

```python
import jax
import jax.numpy as jnp
from jax import lax
from jax.sharding import PartitionSpec as P

BS = 64
PC = 16
NX = 4
NZ = 8
HIGHEST = lax.Precision.HIGHEST
F32 = jnp.float32
BF16 = jnp.bfloat16


def shift_x(step):
    return [(x * NZ + z, (x + step) % NX * NZ + z) for x in range(NX) for z in range(NZ)]


def two_parts(values):
    high = lax.reduce_precision(values, 8, 7)
    return high.astype(BF16), (values - high).astype(BF16)


def body(a_blocks, blk_row, blk_col, drop_mask, prolong, agg_label, inv_diag):
    slot_count = a_blocks.shape[0]
    per_device = prolong.shape[0]
    width = prolong.shape[1]
    col_count = lax.axis_size("col")
    row_index = lax.axis_index("row")
    col_index = lax.axis_index("col")
    span = col_count * per_device
    panel_first = row_index * span
    own_first = panel_first + col_index * per_device

    part = inv_diag.shape[1] // NX
    quarters = inv_diag.reshape(per_device, NX, 1, part).transpose(1, 2, 0, 3)
    quarters = jnp.broadcast_to(quarters, (NX, NZ, per_device, part))
    quarters = quarters.reshape(col_count, per_device, part)
    copies = jnp.broadcast_to(prolong[None], (col_count, per_device, width))
    first = jnp.concatenate([copies, quarters], axis=2)
    first = lax.all_to_all(first, "col", 0, 0, tiled=True).reshape(span, width + part)
    row_panel = first[:, :width]
    inv_own = first[:, width:]
    inv_left = lax.ppermute(inv_own, "col", shift_x(1))
    inv_right = lax.ppermute(inv_own, "col", shift_x(-1))
    inv_far_a = lax.ppermute(inv_left[: span // 2], "col", shift_x(1))
    inv_far_b = lax.ppermute(inv_right[span // 2 :], "col", shift_x(-1))

    labelled = jnp.concatenate(
        [prolong, jnp.broadcast_to(agg_label.astype(BF16)[:, None], (per_device, 128))], axis=1
    )
    col_panel = lax.all_gather(labelled, "row", axis=0, tiled=True)

    keep = (drop_mask == 1) | (blk_row == blk_col)
    local_row = blk_row - panel_first
    matrices = a_blocks.reshape(slot_count, BS, BS)

    pick = (local_row[:, None] == jnp.arange(span)[None, :]) & ~keep[:, None]
    row_blocks = jnp.dot(pick.astype(BF16), row_panel, preferred_element_type=F32).astype(BF16)
    drop_terms = jnp.einsum(
        "sij,sjk->sik",
        matrices,
        row_blocks.reshape(slot_count, BS, PC),
        preferred_element_type=F32,
    ).reshape(slot_count, width)
    place = (jnp.arange(span)[:, None] == local_row[None, :]).astype(BF16)
    parts = jnp.concatenate(two_parts(drop_terms), axis=0)
    sums = jnp.dot(jnp.concatenate([place, place], axis=1), parts, preferred_element_type=F32)
    sums = sums.reshape(col_count, per_device, width)
    arrived = lax.all_to_all(sums, "col", 0, 0, tiled=True)
    lumped = jnp.sum(arrived.reshape(col_count, per_device, width), axis=0)
    scaled_lumped = jnp.einsum(
        "eij,ejk->eik",
        inv_diag.astype(F32).reshape(per_device, BS, BS),
        lumped.reshape(per_device, BS, PC),
        precision=HIGHEST,
    ).reshape(per_device, width)

    col_place = blk_col // span * per_device + blk_col % per_device
    pick = col_place[:, None] == jnp.arange(col_panel.shape[0])[None, :]
    picked = jnp.dot(pick.astype(BF16), col_panel, preferred_element_type=F32)
    col_label = picked[:, width]
    col_blocks = (picked[:, :width] * keep[:, None].astype(F32)).astype(BF16)
    kept_terms = jnp.einsum(
        "sij,sjk->sik",
        matrices,
        col_blocks.reshape(slot_count, BS, PC),
        preferred_element_type=F32,
    ).reshape(slot_count, width)
    col_run = blk_col // per_device
    row_run = blk_row // per_device
    same_group = (
        (blk_row[:, None] == blk_row[None, :])
        & (col_run[:, None] == col_run[None, :])
        & (col_label[:, None] == col_label[None, :])
    ).astype(BF16)
    parts = jnp.concatenate(two_parts(kept_terms), axis=0)
    grouped = jnp.dot(
        jnp.concatenate([same_group, same_group], axis=1), parts, preferred_element_type=F32
    )

    pick = (local_row[:, None] == jnp.arange(span)[None, :]).astype(BF16)
    parts = [half.reshape(slot_count, BS, PC) for half in two_parts(grouped)]
    parts = jnp.concatenate(parts, axis=2)

    def quarter(pieces):
        taken = None
        for first_row, piece in pieces:
            chosen = pick[:, first_row : first_row + piece.shape[0]]
            term = jnp.dot(chosen, piece, preferred_element_type=F32)
            taken = term if taken is None else taken + term
        taken = taken.astype(BF16).reshape(slot_count, BS // NX, BS)
        terms = jnp.einsum("sij,sjk->sik", taken, parts, preferred_element_type=F32)
        terms = terms[:, :, :PC] + terms[:, :, PC:]
        return terms.reshape(slot_count, width // NX)

    by_distance = [
        quarter([(0, inv_own)]),
        quarter([(0, inv_right)]),
        quarter([(0, inv_far_a), (span // 2, inv_far_b)]),
        quarter([(0, inv_left)]),
    ]
    col_x = col_index // NZ
    in_order = []
    for q in range(NX):
        value = by_distance[0]
        for distance in range(1, NX):
            value = jnp.where((q - col_x) % NX == distance, by_distance[distance], value)
        in_order.append(value)
    coarse = jnp.concatenate(in_order, axis=1)

    target = (
        (blk_row[:, None] == own_first + jnp.arange(per_device)[None, :])
        & (col_run == row_run)[:, None]
        & (col_label[:, None] == agg_label.astype(F32)[None, :])
    )
    return coarse + jnp.dot(target.astype(F32), scaled_lumped, precision=HIGHEST)


def solution(mesh):
    return jax.shard_map(
        body,
        mesh=mesh,
        in_specs=(
            P(("row", "col"), None),
            P(("row", "col")),
            P(("row", "col")),
            P(("row", "col")),
            P(("row", "col"), None),
            P(("row", "col")),
            P(("row", "col"), None),
        ),
        out_specs=P(("row", "col"), None),
        check_vma=False,
    )
```

```python
import jax
import jax.numpy as jnp
from jax import lax
from jax.sharding import PartitionSpec as P

BS = 64
PC = 16
NX = 4
NZ = 8
HIGHEST = lax.Precision.HIGHEST
F32 = jnp.float32
BF16 = jnp.bfloat16

X_GROUPS = [[x * NZ + z for x in range(NX)] for z in range(NZ)]
Z_GROUPS = [[x * NZ + z for z in range(NZ)] for x in range(NX)]


def spread(values, groups):
    count = len(groups[0])
    copies = jnp.broadcast_to(values[None], (count,) + values.shape)
    moved = lax.all_to_all(copies, "col", 0, 0, axis_index_groups=groups, tiled=True)
    return moved.reshape((count * values.shape[0],) + values.shape[1:])


def shift_x(step):
    return [(x * NZ + z, (x + step) % NX * NZ + z) for x in range(NX) for z in range(NZ)]


def two_parts(values):
    high = lax.reduce_precision(values, 8, 7)
    return high.astype(BF16), (values - high).astype(BF16)


def body(a_blocks, blk_row, blk_col, drop_mask, prolong, agg_label, inv_diag):
    slot_count = a_blocks.shape[0]
    per_device = prolong.shape[0]
    width = prolong.shape[1]
    col_count = lax.axis_size("col")
    row_index = lax.axis_index("row")
    col_index = lax.axis_index("col")
    span = col_count * per_device
    panel_first = row_index * span
    own_first = panel_first + col_index * per_device

    copies = [jnp.broadcast_to(part[None], (NZ,) + part.shape) for part in (prolong, inv_diag)]
    both = lax.all_to_all(
        jnp.concatenate(copies, axis=2), "col", 0, 0, axis_index_groups=Z_GROUPS, tiled=True
    ).reshape(NZ * per_device, width + inv_diag.shape[1])
    row_panel = spread(both[:, :width], X_GROUPS)
    inv_parts = [both[:, width:]]
    for k in (1, 2, 3):
        inv_parts.append(lax.ppermute(inv_parts[0], "col", shift_x(k)))

    labelled = jnp.concatenate(
        [prolong, jnp.broadcast_to(agg_label.astype(BF16)[:, None], (per_device, 128))], axis=1
    )
    col_panel = lax.all_gather(labelled, "row", axis=0, tiled=True)

    keep = (drop_mask == 1) | (blk_row == blk_col)
    local_row = blk_row - panel_first
    matrices = a_blocks.reshape(slot_count, BS, BS)

    pick = (local_row[:, None] == jnp.arange(span)[None, :]) & ~keep[:, None]
    row_blocks = jnp.dot(pick.astype(BF16), row_panel, preferred_element_type=F32).astype(BF16)
    drop_terms = jnp.einsum(
        "sij,sjk->sik",
        matrices,
        row_blocks.reshape(slot_count, BS, PC),
        preferred_element_type=F32,
    ).reshape(slot_count, width)
    place = (jnp.arange(span)[:, None] == local_row[None, :]).astype(BF16)
    parts = jnp.concatenate(two_parts(drop_terms), axis=0)
    sums = jnp.dot(jnp.concatenate([place, place], axis=1), parts, preferred_element_type=F32)
    sums = sums.reshape(col_count, per_device, width)
    arrived = lax.all_to_all(sums, "col", 0, 0, tiled=True)
    lumped = jnp.sum(arrived.reshape(col_count, per_device, width), axis=0)
    scaled_lumped = jnp.einsum(
        "eij,ejk->eik",
        inv_diag.astype(F32).reshape(per_device, BS, BS),
        lumped.reshape(per_device, BS, PC),
        precision=HIGHEST,
    ).reshape(per_device, width)

    col_place = blk_col // span * per_device + blk_col % per_device
    pick = col_place[:, None] == jnp.arange(col_panel.shape[0])[None, :]
    picked = jnp.dot(pick.astype(BF16), col_panel, preferred_element_type=F32)
    col_label = picked[:, width]
    col_blocks = (picked[:, :width] * keep[:, None].astype(F32)).astype(BF16)
    kept_terms = jnp.einsum(
        "sij,sjk->sik",
        matrices,
        col_blocks.reshape(slot_count, BS, PC),
        preferred_element_type=F32,
    ).reshape(slot_count, width)
    col_run = blk_col // per_device
    row_run = blk_row // per_device
    same_group = (
        (blk_row[:, None] == blk_row[None, :])
        & (col_run[:, None] == col_run[None, :])
        & (col_label[:, None] == col_label[None, :])
    ).astype(BF16)
    parts = jnp.concatenate(two_parts(kept_terms), axis=0)
    grouped = jnp.dot(
        jnp.concatenate([same_group, same_group], axis=1), parts, preferred_element_type=F32
    )

    part_rows = NZ * per_device
    row_x = local_row // part_rows
    inverse = None
    for k in (0, 1, 2, 3):
        at = jnp.where((col_index // NZ - row_x) % NX == k, local_row % part_rows, -1)
        pick = (at[:, None] == jnp.arange(part_rows)[None, :]).astype(BF16)
        piece = jnp.dot(pick, inv_parts[k], preferred_element_type=F32)
        inverse = piece if inverse is None else inverse + piece
    inverse = inverse.astype(BF16)
    inverse = inverse.reshape(slot_count, BS, BS)
    parts = [part.reshape(slot_count, BS, PC) for part in two_parts(grouped)]
    coarse = jnp.einsum(
        "sij,sjk->sik", inverse, jnp.concatenate(parts, axis=2), preferred_element_type=F32
    )
    coarse = (coarse[:, :, :PC] + coarse[:, :, PC:]).reshape(slot_count, width)

    target = (
        (blk_row[:, None] == own_first + jnp.arange(per_device)[None, :])
        & (col_run == row_run)[:, None]
        & (col_label[:, None] == agg_label.astype(F32)[None, :])
    )
    return coarse + jnp.dot(target.astype(F32), scaled_lumped, precision=HIGHEST)


def solution(mesh):
    return jax.shard_map(
        body,
        mesh=mesh,
        in_specs=(
            P(("row", "col"), None),
            P(("row", "col")),
            P(("row", "col")),
            P(("row", "col")),
            P(("row", "col"), None),
            P(("row", "col")),
            P(("row", "col"), None),
        ),
        out_specs=P(("row", "col"), None),
        check_vma=False,
    )
```

```python
import jax
import jax.numpy as jnp
from jax import lax
from jax.sharding import PartitionSpec as P

BS = 64
PC = 16
NX = 4
NZ = 8
HIGHEST = lax.Precision.HIGHEST
F32 = jnp.float32
BF16 = jnp.bfloat16

X_GROUPS = [[x * NZ + z for x in range(NX)] for z in range(NZ)]
Z_GROUPS = [[x * NZ + z for z in range(NZ)] for x in range(NX)]


def spread(values, groups):
    count = len(groups[0])
    copies = jnp.broadcast_to(values[None], (count,) + values.shape)
    moved = lax.all_to_all(copies, "col", 0, 0, axis_index_groups=groups, tiled=True)
    return moved.reshape((count * values.shape[0],) + values.shape[1:])


def shift_x(step):
    return [(x * NZ + z, (x + step) % NX * NZ + z) for x in range(NX) for z in range(NZ)]


def two_parts(values):
    high = lax.reduce_precision(values, 8, 7)
    return high.astype(BF16), (values - high).astype(BF16)


def body(a_blocks, blk_row, blk_col, drop_mask, prolong, agg_label, inv_diag):
    slot_count = a_blocks.shape[0]
    per_device = prolong.shape[0]
    width = prolong.shape[1]
    col_count = lax.axis_size("col")
    row_index = lax.axis_index("row")
    col_index = lax.axis_index("col")
    span = col_count * per_device
    panel_first = row_index * span
    own_first = panel_first + col_index * per_device

    copies = [jnp.broadcast_to(part[None], (NZ,) + part.shape) for part in (prolong, inv_diag)]
    both = lax.all_to_all(
        jnp.concatenate(copies, axis=2), "col", 0, 0, axis_index_groups=Z_GROUPS, tiled=True
    ).reshape(NZ * per_device, width + inv_diag.shape[1])
    row_panel = spread(both[:, :width], X_GROUPS)
    inv_own = both[:, width:]
    half = inv_own.shape[0] // 2
    inv_left = lax.ppermute(inv_own, "col", shift_x(1))
    inv_right = lax.ppermute(inv_own, "col", shift_x(-1))
    inv_far_a = lax.ppermute(inv_left[:half], "col", shift_x(1))
    inv_far_b = lax.ppermute(inv_right[half:], "col", shift_x(-1))
    inv_parts = (
        (0, 0, inv_own),
        (1, 0, inv_left),
        (3, 0, inv_right),
        (2, 0, inv_far_a),
        (2, half, inv_far_b),
    )

    labelled = jnp.concatenate(
        [prolong, jnp.broadcast_to(agg_label.astype(BF16)[:, None], (per_device, 128))], axis=1
    )
    col_panel = lax.all_gather(labelled, "row", axis=0, tiled=True)

    keep = (drop_mask == 1) | (blk_row == blk_col)
    local_row = blk_row - panel_first
    matrices = a_blocks.reshape(slot_count, BS, BS)

    pick = (local_row[:, None] == jnp.arange(span)[None, :]) & ~keep[:, None]
    row_blocks = jnp.dot(pick.astype(BF16), row_panel, preferred_element_type=F32).astype(BF16)
    drop_terms = jnp.einsum(
        "sij,sjk->sik",
        matrices,
        row_blocks.reshape(slot_count, BS, PC),
        preferred_element_type=F32,
    ).reshape(slot_count, width)
    place = (jnp.arange(span)[:, None] == local_row[None, :]).astype(BF16)
    parts = jnp.concatenate(two_parts(drop_terms), axis=0)
    sums = jnp.dot(jnp.concatenate([place, place], axis=1), parts, preferred_element_type=F32)
    sums = sums.reshape(col_count, per_device, width)
    arrived = lax.all_to_all(sums, "col", 0, 0, tiled=True)
    lumped = jnp.sum(arrived.reshape(col_count, per_device, width), axis=0)
    scaled_lumped = jnp.einsum(
        "eij,ejk->eik",
        inv_diag.astype(F32).reshape(per_device, BS, BS),
        lumped.reshape(per_device, BS, PC),
        precision=HIGHEST,
    ).reshape(per_device, width)

    col_place = blk_col // span * per_device + blk_col % per_device
    pick = col_place[:, None] == jnp.arange(col_panel.shape[0])[None, :]
    picked = jnp.dot(pick.astype(BF16), col_panel, preferred_element_type=F32)
    col_label = picked[:, width]
    col_blocks = (picked[:, :width] * keep[:, None].astype(F32)).astype(BF16)
    kept_terms = jnp.einsum(
        "sij,sjk->sik",
        matrices,
        col_blocks.reshape(slot_count, BS, PC),
        preferred_element_type=F32,
    ).reshape(slot_count, width)
    col_run = blk_col // per_device
    row_run = blk_row // per_device
    same_group = (
        (blk_row[:, None] == blk_row[None, :])
        & (col_run[:, None] == col_run[None, :])
        & (col_label[:, None] == col_label[None, :])
    ).astype(BF16)
    parts = jnp.concatenate(two_parts(kept_terms), axis=0)
    grouped = jnp.dot(
        jnp.concatenate([same_group, same_group], axis=1), parts, preferred_element_type=F32
    )

    part_rows = NZ * per_device
    row_x = local_row // part_rows
    inverse = None
    for distance, first_row, rows in inv_parts:
        at = jnp.where((col_index // NZ - row_x) % NX == distance, local_row % part_rows, -1)
        pick = (at[:, None] == first_row + jnp.arange(rows.shape[0])[None, :]).astype(BF16)
        piece = jnp.dot(pick, rows, preferred_element_type=F32)
        inverse = piece if inverse is None else inverse + piece
    inverse = inverse.astype(BF16)
    inverse = inverse.reshape(slot_count, BS, BS)
    parts = [part.reshape(slot_count, BS, PC) for part in two_parts(grouped)]
    coarse = jnp.einsum(
        "sij,sjk->sik", inverse, jnp.concatenate(parts, axis=2), preferred_element_type=F32
    )
    coarse = (coarse[:, :, :PC] + coarse[:, :, PC:]).reshape(slot_count, width)

    target = (
        (blk_row[:, None] == own_first + jnp.arange(per_device)[None, :])
        & (col_run == row_run)[:, None]
        & (col_label[:, None] == agg_label.astype(F32)[None, :])
    )
    return coarse + jnp.dot(target.astype(F32), scaled_lumped, precision=HIGHEST)


def solution(mesh):
    return jax.shard_map(
        body,
        mesh=mesh,
        in_specs=(
            P(("row", "col"), None),
            P(("row", "col")),
            P(("row", "col")),
            P(("row", "col")),
            P(("row", "col"), None),
            P(("row", "col")),
            P(("row", "col"), None),
        ),
        out_specs=P(("row", "col"), None),
        check_vma=False,
    )
```

```python
import jax
import jax.numpy as jnp
from jax import lax
from jax.sharding import PartitionSpec as P

BS = 64
PC = 16
NX = 4
NZ = 8
HIGHEST = lax.Precision.HIGHEST
F32 = jnp.float32
BF16 = jnp.bfloat16

X_GROUPS = [[x * NZ + z for x in range(NX)] for z in range(NZ)]
Z_GROUPS = [[x * NZ + z for z in range(NZ)] for x in range(NX)]


def spread(values, groups):
    count = len(groups[0])
    copies = jnp.broadcast_to(values[None], (count,) + values.shape)
    moved = lax.all_to_all(copies, "col", 0, 0, axis_index_groups=groups, tiled=True)
    return moved.reshape((count * values.shape[0],) + values.shape[1:])


def shift_x(step):
    return [(x * NZ + z, (x + step) % NX * NZ + z) for x in range(NX) for z in range(NZ)]


def two_parts(values):
    high = lax.reduce_precision(values, 8, 7)
    return high.astype(BF16), (values - high).astype(BF16)


def body(a_blocks, blk_row, blk_col, drop_mask, prolong, agg_label, inv_diag):
    slot_count = a_blocks.shape[0]
    per_device = prolong.shape[0]
    width = prolong.shape[1]
    col_count = lax.axis_size("col")
    row_index = lax.axis_index("row")
    col_index = lax.axis_index("col")
    span = col_count * per_device
    panel_first = row_index * span
    own_first = panel_first + col_index * per_device

    both = spread(jnp.concatenate([prolong, inv_diag], axis=1), Z_GROUPS)

    labelled = jnp.concatenate(
        [prolong, jnp.broadcast_to(agg_label.astype(BF16)[:, None], (per_device, 128))], axis=1
    )
    col_panel = lax.all_gather(labelled, "row", axis=0, tiled=True)

    both, col_panel, a_blocks, blk_row, blk_col, drop_mask, own_label, own_inv = (
        lax.optimization_barrier(
            (both, col_panel, a_blocks, blk_row, blk_col, drop_mask, agg_label, inv_diag)
        )
    )
    row_panel = spread(both[:, :width], X_GROUPS)
    inv_own = both[:, width:]
    half = inv_own.shape[0] // 2
    inv_left = lax.ppermute(inv_own, "col", shift_x(1))
    inv_right = lax.ppermute(inv_own, "col", shift_x(-1))
    inv_far_a = lax.ppermute(inv_left[:half], "col", shift_x(1))
    inv_far_b = lax.ppermute(inv_right[half:], "col", shift_x(-1))
    inv_parts = (
        (0, 0, inv_own),
        (1, 0, inv_left),
        (3, 0, inv_right),
        (2, 0, inv_far_a),
        (2, half, inv_far_b),
    )

    keep = (drop_mask == 1) | (blk_row == blk_col)
    local_row = blk_row - panel_first
    matrices = a_blocks.reshape(slot_count, BS, BS)

    pick = (local_row[:, None] == jnp.arange(span)[None, :]) & ~keep[:, None]
    row_blocks = jnp.dot(pick.astype(BF16), row_panel, preferred_element_type=F32).astype(BF16)
    drop_terms = jnp.einsum(
        "sij,sjk->sik",
        matrices,
        row_blocks.reshape(slot_count, BS, PC),
        preferred_element_type=F32,
    ).reshape(slot_count, width)
    place = (jnp.arange(span)[:, None] == local_row[None, :]).astype(BF16)
    parts = jnp.concatenate(two_parts(drop_terms), axis=0)
    sums = jnp.dot(jnp.concatenate([place, place], axis=1), parts, preferred_element_type=F32)
    sums = sums.reshape(col_count, per_device, width)
    arrived = lax.all_to_all(sums, "col", 0, 0, tiled=True)
    lumped = jnp.sum(arrived.reshape(col_count, per_device, width), axis=0)
    scaled_lumped = jnp.einsum(
        "eij,ejk->eik",
        own_inv.astype(F32).reshape(per_device, BS, BS),
        lumped.reshape(per_device, BS, PC),
        precision=HIGHEST,
    ).reshape(per_device, width)

    col_place = blk_col // span * per_device + blk_col % per_device
    pick = col_place[:, None] == jnp.arange(col_panel.shape[0])[None, :]
    picked = jnp.dot(pick.astype(BF16), col_panel, preferred_element_type=F32)
    col_label = picked[:, width]
    col_blocks = (picked[:, :width] * keep[:, None].astype(F32)).astype(BF16)
    kept_terms = jnp.einsum(
        "sij,sjk->sik",
        matrices,
        col_blocks.reshape(slot_count, BS, PC),
        preferred_element_type=F32,
    ).reshape(slot_count, width)
    col_run = blk_col // per_device
    row_run = blk_row // per_device
    same_group = (
        (blk_row[:, None] == blk_row[None, :])
        & (col_run[:, None] == col_run[None, :])
        & (col_label[:, None] == col_label[None, :])
    ).astype(BF16)
    parts = jnp.concatenate(two_parts(kept_terms), axis=0)
    grouped = jnp.dot(
        jnp.concatenate([same_group, same_group], axis=1), parts, preferred_element_type=F32
    )

    part_rows = NZ * per_device
    row_x = local_row // part_rows
    inverse = None
    for distance, first_row, rows in inv_parts:
        at = jnp.where((col_index // NZ - row_x) % NX == distance, local_row % part_rows, -1)
        pick = ((at - first_row)[:, None] == jnp.arange(rows.shape[0])[None, :]).astype(BF16)
        piece = jnp.dot(pick, rows, preferred_element_type=F32)
        inverse = piece if inverse is None else inverse + piece
    inverse = inverse.astype(BF16)
    inverse = inverse.reshape(slot_count, BS, BS)
    parts = [part.reshape(slot_count, BS, PC) for part in two_parts(grouped)]
    coarse = jnp.einsum(
        "sij,sjk->sik", inverse, jnp.concatenate(parts, axis=2), preferred_element_type=F32
    )
    coarse = (coarse[:, :, :PC] + coarse[:, :, PC:]).reshape(slot_count, width)

    target = (
        (blk_row[:, None] == own_first + jnp.arange(per_device)[None, :])
        & (col_run == row_run)[:, None]
        & (col_label[:, None] == own_label.astype(F32)[None, :])
    )
    target = target.astype(BF16)
    parts = jnp.concatenate(two_parts(scaled_lumped), axis=0)
    return coarse + jnp.dot(
        jnp.concatenate([target, target], axis=1), parts, preferred_element_type=F32
    )


def solution(mesh):
    return jax.shard_map(
        body,
        mesh=mesh,
        in_specs=(
            P(("row", "col"), None),
            P(("row", "col")),
            P(("row", "col")),
            P(("row", "col")),
            P(("row", "col"), None),
            P(("row", "col")),
            P(("row", "col"), None),
        ),
        out_specs=P(("row", "col"), None),
        check_vma=False,
    )
```

```python
import jax
import jax.numpy as jnp
from jax import lax
from jax.sharding import PartitionSpec as P

BS = 64
PC = 16
NX = 4
NZ = 8
HIGHEST = lax.Precision.HIGHEST
F32 = jnp.float32
BF16 = jnp.bfloat16
F16 = jnp.float16

X_GROUPS = [[x * NZ + z for x in range(NX)] for z in range(NZ)]
Z_GROUPS = [[x * NZ + z for z in range(NZ)] for x in range(NX)]


def spread(values, groups):
    count = len(groups[0])
    copies = jnp.broadcast_to(values[None], (count,) + values.shape)
    moved = lax.all_to_all(copies, "col", 0, 0, axis_index_groups=groups, tiled=True)
    return moved.reshape((count * values.shape[0],) + values.shape[1:])


def shift_x(step):
    return [(x * NZ + z, (x + step) % NX * NZ + z) for x in range(NX) for z in range(NZ)]


def power_of_two(exponent):
    return lax.reduce_precision(jnp.exp2(exponent), 8, 7)


def two_parts(values):
    high = lax.reduce_precision(values, 8, 7)
    return high.astype(BF16), (values - high).astype(BF16)


def body(a_blocks, blk_row, blk_col, drop_mask, prolong, agg_label, inv_diag):
    slot_count = a_blocks.shape[0]
    per_device = prolong.shape[0]
    width = prolong.shape[1]
    col_count = lax.axis_size("col")
    row_index = lax.axis_index("row")
    col_index = lax.axis_index("col")
    span = col_count * per_device
    panel_first = row_index * span
    own_first = panel_first + col_index * per_device

    both = spread(jnp.concatenate([prolong, inv_diag], axis=1), Z_GROUPS)

    labelled = jnp.concatenate(
        [prolong, jnp.broadcast_to(agg_label.astype(BF16)[:, None], (per_device, 128))], axis=1
    )
    col_panel = lax.all_gather(labelled, "row", axis=0, tiled=True)

    both, col_panel, a_blocks, blk_row, blk_col, drop_mask, own_label, own_inv = (
        lax.optimization_barrier(
            (both, col_panel, a_blocks, blk_row, blk_col, drop_mask, agg_label, inv_diag)
        )
    )
    row_panel = spread(both[:, :width], X_GROUPS)
    inv_parts = [both[:, width:]]
    for k in (1, 2, 3):
        inv_parts.append(lax.ppermute(inv_parts[0], "col", shift_x(k)))

    keep = (drop_mask == 1) | (blk_row == blk_col)
    local_row = blk_row - panel_first
    matrices = a_blocks.reshape(slot_count, BS, BS)

    pick = (local_row[:, None] == jnp.arange(span)[None, :]) & ~keep[:, None]
    row_blocks = jnp.dot(pick.astype(BF16), row_panel, preferred_element_type=F32).astype(BF16)
    drop_terms = jnp.einsum(
        "sij,sjk->sik",
        matrices,
        row_blocks.reshape(slot_count, BS, PC),
        preferred_element_type=F32,
    ).reshape(slot_count, width)
    drop_parts = jnp.concatenate(two_parts(drop_terms), axis=0)
    largest = jnp.max(jnp.abs(drop_terms), axis=1)
    remote = (local_row // per_device != col_index) & ~keep
    place = (jnp.arange(span)[:, None] == local_row[None, :]) & remote[None, :]
    largest = jnp.max(jnp.where(place, largest[None, :], 0.0), axis=1)
    exponent = jnp.floor(jnp.log2(jnp.clip(largest, 1e-30, 1e30)))
    place = jnp.where(place, power_of_two(-exponent)[:, None], 0.0).astype(BF16)
    sums = jnp.dot(jnp.concatenate([place, place], axis=1), drop_parts, preferred_element_type=F32)
    sums = jnp.concatenate(
        [sums.astype(F16), jnp.broadcast_to(exponent.astype(F16)[:, None], (span, 128))], axis=1
    ).reshape(col_count, per_device, width + 128)
    arrived = lax.all_to_all(sums, "col", 0, 0, tiled=True)
    arrived = arrived.reshape(col_count, per_device, width + 128)
    factor = power_of_two(arrived[:, :, width:].astype(F32))[:, :, :1]
    own = (blk_row[None, :] == own_first + jnp.arange(per_device)[:, None]) & ~keep[None, :]
    own = own.astype(BF16)
    lumped = jnp.dot(jnp.concatenate([own, own], axis=1), drop_parts, preferred_element_type=F32)
    lumped = lumped + jnp.sum(arrived[:, :, :width].astype(F32) * factor, axis=0)
    scaled_lumped = jnp.einsum(
        "eij,ejk->eik",
        own_inv.astype(F32).reshape(per_device, BS, BS),
        lumped.reshape(per_device, BS, PC),
        precision=HIGHEST,
    ).reshape(per_device, width)

    col_place = blk_col // span * per_device + blk_col % per_device
    pick = col_place[:, None] == jnp.arange(col_panel.shape[0])[None, :]
    picked = jnp.dot(pick.astype(BF16), col_panel, preferred_element_type=F32)
    col_label = picked[:, width]
    col_blocks = (picked[:, :width] * keep[:, None].astype(F32)).astype(BF16)
    kept_terms = jnp.einsum(
        "sij,sjk->sik",
        matrices,
        col_blocks.reshape(slot_count, BS, PC),
        preferred_element_type=F32,
    ).reshape(slot_count, width)
    col_run = blk_col // per_device
    row_run = blk_row // per_device
    same_group = (
        (blk_row[:, None] == blk_row[None, :])
        & (col_run[:, None] == col_run[None, :])
        & (col_label[:, None] == col_label[None, :])
    ).astype(BF16)
    parts = jnp.concatenate(two_parts(kept_terms), axis=0)
    grouped = jnp.dot(
        jnp.concatenate([same_group, same_group], axis=1), parts, preferred_element_type=F32
    )

    part_rows = NZ * per_device
    row_x = local_row // part_rows
    inverse = None
    for k in range(NX):
        at = jnp.where((col_index // NZ - row_x) % NX == k, local_row % part_rows, -1)
        pick = (at[:, None] == jnp.arange(part_rows)[None, :]).astype(BF16)
        piece = jnp.dot(pick, inv_parts[k], preferred_element_type=F32)
        inverse = piece if inverse is None else inverse + piece
    inverse = inverse.astype(BF16)
    inverse = inverse.reshape(slot_count, BS, BS)
    parts = [part.reshape(slot_count, BS, PC) for part in two_parts(grouped)]
    coarse = jnp.einsum(
        "sij,sjk->sik", inverse, jnp.concatenate(parts, axis=2), preferred_element_type=F32
    )
    coarse = (coarse[:, :, :PC] + coarse[:, :, PC:]).reshape(slot_count, width)

    target = (
        (blk_row[:, None] == own_first + jnp.arange(per_device)[None, :])
        & (col_run == row_run)[:, None]
        & (col_label[:, None] == own_label.astype(F32)[None, :])
    )
    target = target.astype(BF16)
    parts = jnp.concatenate(two_parts(scaled_lumped), axis=0)
    return coarse + jnp.dot(
        jnp.concatenate([target, target], axis=1), parts, preferred_element_type=F32
    )


def solution(mesh):
    return jax.shard_map(
        body,
        mesh=mesh,
        in_specs=(
            P(("row", "col"), None),
            P(("row", "col")),
            P(("row", "col")),
            P(("row", "col")),
            P(("row", "col"), None),
            P(("row", "col")),
            P(("row", "col"), None),
        ),
        out_specs=P(("row", "col"), None),
        check_vma=False,
    )
```

```python
import jax
import jax.numpy as jnp
from jax import lax
from jax.sharding import PartitionSpec as P

BS = 64
PC = 16
NX = 4
NZ = 8
HIGHEST = lax.Precision.HIGHEST
F32 = jnp.float32
BF16 = jnp.bfloat16
F16 = jnp.float16

X_GROUPS = [[x * NZ + z for x in range(NX)] for z in range(NZ)]
Z_GROUPS = [[x * NZ + z for z in range(NZ)] for x in range(NX)]


def spread(values, groups):
    count = len(groups[0])
    copies = jnp.broadcast_to(values[None], (count,) + values.shape)
    moved = lax.all_to_all(copies, "col", 0, 0, axis_index_groups=groups, tiled=True)
    return moved.reshape((count * values.shape[0],) + values.shape[1:])


def shift_x(step):
    return [(x * NZ + z, (x + step) % NX * NZ + z) for x in range(NX) for z in range(NZ)]


def power_of_two(exponent):
    return lax.reduce_precision(jnp.exp2(exponent), 8, 7)


def two_parts(values):
    high = lax.reduce_precision(values, 8, 7)
    return high.astype(BF16), (values - high).astype(BF16)


def body(a_blocks, blk_row, blk_col, drop_mask, prolong, agg_label, inv_diag):
    slot_count = a_blocks.shape[0]
    per_device = prolong.shape[0]
    width = prolong.shape[1]
    col_count = lax.axis_size("col")
    row_index = lax.axis_index("row")
    col_index = lax.axis_index("col")
    span = col_count * per_device
    panel_first = row_index * span
    own_first = panel_first + col_index * per_device

    lead = 128
    labelled = jnp.concatenate(
        [jnp.broadcast_to(agg_label.astype(BF16)[:, None], (per_device, lead)), prolong], axis=1
    )
    joined = jnp.concatenate([prolong, inv_diag], axis=1)
    copies = jnp.broadcast_to(joined[None], (NZ,) + joined.shape)
    both = lax.all_to_all(copies, "col", 0, 0, axis_index_groups=Z_GROUPS, tiled=True)
    both = both.reshape(NZ * per_device, joined.shape[1])

    col_panel = lax.all_gather(labelled, "row", axis=0, tiled=True)

    both, col_panel, a_blocks, blk_row, blk_col, drop_mask, own_label, own_inv = (
        lax.optimization_barrier(
            (both, col_panel, a_blocks, blk_row, blk_col, drop_mask, agg_label, inv_diag)
        )
    )
    row_panel = spread(both[:, :width], X_GROUPS)
    inv_parts = [both[:, width:]]
    for k in (1, 2, 3):
        inv_parts.append(lax.ppermute(inv_parts[0], "col", shift_x(k)))

    keep = (drop_mask == 1) | (blk_row == blk_col)
    local_row = blk_row - panel_first
    matrices = a_blocks.reshape(slot_count, BS, BS)

    pick = (local_row[:, None] == jnp.arange(span)[None, :]) & ~keep[:, None]
    row_blocks = jnp.dot(pick.astype(BF16), row_panel, preferred_element_type=F32).astype(BF16)
    drop_terms = jnp.einsum(
        "sij,sjk->sik",
        matrices,
        row_blocks.reshape(slot_count, BS, PC),
        preferred_element_type=F32,
    ).reshape(slot_count, width)
    drop_parts = jnp.concatenate(two_parts(drop_terms), axis=0)
    largest = jnp.max(jnp.abs(drop_terms), axis=1)
    remote = (local_row // per_device != col_index) & ~keep
    place = (jnp.arange(span)[:, None] == local_row[None, :]) & remote[None, :]
    largest = jnp.max(jnp.where(place, largest[None, :], 0.0), axis=1)
    exponent = jnp.floor(jnp.log2(jnp.clip(largest, 1e-30, 1e30)))
    place = jnp.where(place, power_of_two(-exponent)[:, None], 0.0).astype(BF16)
    sums = jnp.dot(jnp.concatenate([place, place], axis=1), drop_parts, preferred_element_type=F32)
    sums = jnp.concatenate(
        [sums.astype(F16), jnp.broadcast_to(exponent.astype(F16)[:, None], (span, 128))], axis=1
    ).reshape(col_count, per_device, width + 128)
    arrived = lax.all_to_all(sums, "col", 0, 0, tiled=True)
    arrived = arrived.reshape(col_count, per_device, width + 128)
    factor = power_of_two(arrived[:, :, width:].astype(F32))[:, :, :1]
    own = (blk_row[None, :] == own_first + jnp.arange(per_device)[:, None]) & ~keep[None, :]
    own = own.astype(BF16)
    lumped = jnp.dot(jnp.concatenate([own, own], axis=1), drop_parts, preferred_element_type=F32)
    lumped = lumped + jnp.sum(arrived[:, :, :width].astype(F32) * factor, axis=0)
    scaled_lumped = jnp.einsum(
        "eij,ejk->eik",
        own_inv.astype(F32).reshape(per_device, BS, BS),
        lumped.reshape(per_device, BS, PC),
        precision=HIGHEST,
    ).reshape(per_device, width)

    col_place = blk_col // span * per_device + blk_col % per_device
    pick = col_place[:, None] == jnp.arange(col_panel.shape[0])[None, :]
    picked = jnp.dot(pick.astype(BF16), col_panel, preferred_element_type=F32)
    col_label = picked[:, 0]
    col_blocks = (picked[:, lead:] * keep[:, None].astype(F32)).astype(BF16)
    kept_terms = jnp.einsum(
        "sij,sjk->sik",
        matrices,
        col_blocks.reshape(slot_count, BS, PC),
        preferred_element_type=F32,
    ).reshape(slot_count, width)
    col_run = blk_col // per_device
    row_run = blk_row // per_device
    same_group = (
        (blk_row[:, None] == blk_row[None, :])
        & (col_run[:, None] == col_run[None, :])
        & (col_label[:, None] == col_label[None, :])
    ).astype(BF16)
    parts = jnp.concatenate(two_parts(kept_terms), axis=0)
    grouped = jnp.dot(
        jnp.concatenate([same_group, same_group], axis=1), parts, preferred_element_type=F32
    )

    part_rows = NZ * per_device
    row_x = local_row // part_rows
    inverse = None
    for k in (0, 1, 3, 2):
        at = jnp.where((col_index // NZ - row_x) % NX == k, local_row % part_rows, -1)
        pick = (at[:, None] == jnp.arange(part_rows)[None, :]).astype(BF16)
        piece = jnp.dot(pick, inv_parts[k], preferred_element_type=F32)
        inverse = piece if inverse is None else inverse + piece
    inverse = inverse.astype(BF16)
    inverse = inverse.reshape(slot_count, BS, BS)
    parts = [part.reshape(slot_count, BS, PC) for part in two_parts(grouped)]
    coarse = jnp.einsum(
        "sij,sjk->sik", inverse, jnp.concatenate(parts, axis=2), preferred_element_type=F32
    )
    coarse = (coarse[:, :, :PC] + coarse[:, :, PC:]).reshape(slot_count, width)

    target = (
        (blk_row[:, None] == own_first + jnp.arange(per_device)[None, :])
        & (col_run == row_run)[:, None]
        & (col_label[:, None] == own_label.astype(F32)[None, :])
    )
    target = target.astype(BF16)
    parts = jnp.concatenate(two_parts(scaled_lumped), axis=0)
    return coarse + jnp.dot(
        jnp.concatenate([target, target], axis=1), parts, preferred_element_type=F32
    )


def solution(mesh):
    return jax.shard_map(
        body,
        mesh=mesh,
        in_specs=(
            P(("row", "col"), None),
            P(("row", "col")),
            P(("row", "col")),
            P(("row", "col")),
            P(("row", "col"), None),
            P(("row", "col")),
            P(("row", "col"), None),
        ),
        out_specs=P(("row", "col"), None),
        check_vma=False,
    )
```

```python
import jax
import jax.numpy as jnp
from jax import lax
from jax.sharding import PartitionSpec as P

BS = 64
PC = 16
NX = 4
NZ = 8
HIGHEST = lax.Precision.HIGHEST
F32 = jnp.float32
BF16 = jnp.bfloat16
F16 = jnp.float16

X_GROUPS = [[x * NZ + z for x in range(NX)] for z in range(NZ)]
Z_GROUPS = [[x * NZ + z for z in range(NZ)] for x in range(NX)]


def spread(values, groups):
    count = len(groups[0])
    copies = jnp.broadcast_to(values[None], (count,) + values.shape)
    moved = lax.all_to_all(copies, "col", 0, 0, axis_index_groups=groups, tiled=True)
    return moved.reshape((count * values.shape[0],) + values.shape[1:])


def shift_x(step):
    return [(x * NZ + z, (x + step) % NX * NZ + z) for x in range(NX) for z in range(NZ)]


def power_of_two(exponent):
    return lax.reduce_precision(jnp.exp2(exponent), 8, 7)


def two_parts(values):
    high = lax.reduce_precision(values, 8, 7)
    return high.astype(BF16), (values - high).astype(BF16)


def body(a_blocks, blk_row, blk_col, drop_mask, prolong, agg_label, inv_diag):
    slot_count = a_blocks.shape[0]
    per_device = prolong.shape[0]
    width = prolong.shape[1]
    col_count = lax.axis_size("col")
    row_index = lax.axis_index("row")
    col_index = lax.axis_index("col")
    span = col_count * per_device
    panel_first = row_index * span
    own_first = panel_first + col_index * per_device

    both = spread(jnp.concatenate([prolong, inv_diag], axis=1), Z_GROUPS)

    labelled = jnp.concatenate(
        [prolong, jnp.broadcast_to(agg_label.astype(BF16)[:, None], (per_device, 128))], axis=1
    )
    col_panel = lax.all_gather(labelled, "row", axis=0, tiled=True)

    both, col_panel, blk_row, blk_col, drop_mask, own_label, own_inv = lax.optimization_barrier(
        (both, col_panel, blk_row, blk_col, drop_mask, agg_label, inv_diag)
    )
    row_panel = spread(both[:, :width], X_GROUPS)
    inv_parts = [both[:, width:]]
    for k in (1, 2, 3):
        inv_parts.append(lax.ppermute(inv_parts[0], "col", shift_x(k)))

    keep = (drop_mask == 1) | (blk_row == blk_col)
    local_row = blk_row - panel_first
    matrices = a_blocks.reshape(slot_count, BS, BS)

    pick = (local_row[:, None] == jnp.arange(span)[None, :]) & ~keep[:, None]
    row_blocks = jnp.dot(pick.astype(BF16), row_panel, preferred_element_type=F32).astype(BF16)
    drop_terms = jnp.einsum(
        "sij,sjk->sik",
        matrices,
        row_blocks.reshape(slot_count, BS, PC),
        preferred_element_type=F32,
    ).reshape(slot_count, width)
    drop_parts = jnp.concatenate(two_parts(drop_terms), axis=0)
    largest = jnp.max(jnp.abs(drop_terms), axis=1)
    remote = (local_row // per_device != col_index) & ~keep
    place = (jnp.arange(span)[:, None] == local_row[None, :]) & remote[None, :]
    largest = jnp.max(jnp.where(place, largest[None, :], 0.0), axis=1)
    exponent = jnp.floor(jnp.log2(jnp.clip(largest, 1e-30, 1e30)))
    place = jnp.where(place, power_of_two(-exponent)[:, None], 0.0).astype(BF16)
    sums = jnp.dot(jnp.concatenate([place, place], axis=1), drop_parts, preferred_element_type=F32)
    sums = jnp.concatenate(
        [sums.astype(F16), jnp.broadcast_to(exponent.astype(F16)[:, None], (span, 128))], axis=1
    ).reshape(col_count, per_device, width + 128)
    arrived = lax.all_to_all(sums, "col", 0, 0, tiled=True)
    arrived = arrived.reshape(col_count, per_device, width + 128)
    factor = power_of_two(arrived[:, :, width:].astype(F32))[:, :, :1]
    own = (blk_row[None, :] == own_first + jnp.arange(per_device)[:, None]) & ~keep[None, :]
    own = own.astype(BF16)
    lumped = jnp.dot(jnp.concatenate([own, own], axis=1), drop_parts, preferred_element_type=F32)
    lumped = lumped + jnp.sum(arrived[:, :, :width].astype(F32) * factor, axis=0)
    scaled_lumped = jnp.einsum(
        "eij,ejk->eik",
        own_inv.astype(F32).reshape(per_device, BS, BS),
        lumped.reshape(per_device, BS, PC),
        precision=HIGHEST,
    ).reshape(per_device, width)

    col_place = blk_col // span * per_device + blk_col % per_device
    pick = col_place[:, None] == jnp.arange(col_panel.shape[0])[None, :]
    picked = jnp.dot(pick.astype(BF16), col_panel, preferred_element_type=F32)
    col_label = picked[:, width]
    col_blocks = (picked[:, :width] * keep[:, None].astype(F32)).astype(BF16)
    kept_terms = jnp.einsum(
        "sij,sjk->sik",
        matrices,
        col_blocks.reshape(slot_count, BS, PC),
        preferred_element_type=F32,
    ).reshape(slot_count, width)
    col_run = blk_col // per_device
    row_run = blk_row // per_device
    same_group = (
        (blk_row[:, None] == blk_row[None, :])
        & (col_run[:, None] == col_run[None, :])
        & (col_label[:, None] == col_label[None, :])
    ).astype(BF16)
    parts = jnp.concatenate(two_parts(kept_terms), axis=0)
    grouped = jnp.dot(
        jnp.concatenate([same_group, same_group], axis=1), parts, preferred_element_type=F32
    )

    part_rows = NZ * per_device
    row_x = local_row // part_rows
    inverse = None
    for k in range(NX):
        at = jnp.where((col_index // NZ - row_x) % NX == k, local_row % part_rows, -1)
        pick = (at[:, None] == jnp.arange(part_rows)[None, :]).astype(BF16)
        piece = jnp.dot(pick, inv_parts[k], preferred_element_type=F32)
        inverse = piece if inverse is None else inverse + piece
    inverse = inverse.astype(BF16)
    inverse = inverse.reshape(slot_count, BS, BS)
    parts = [part.reshape(slot_count, BS, PC) for part in two_parts(grouped)]
    coarse = jnp.einsum(
        "sij,sjk->sik", inverse, jnp.concatenate(parts, axis=2), preferred_element_type=F32
    )
    coarse = (coarse[:, :, :PC] + coarse[:, :, PC:]).reshape(slot_count, width)

    target = (
        (blk_row[:, None] == own_first + jnp.arange(per_device)[None, :])
        & (col_run == row_run)[:, None]
        & (col_label[:, None] == own_label.astype(F32)[None, :])
    )
    target = target.astype(BF16)
    parts = jnp.concatenate(two_parts(scaled_lumped), axis=0)
    return coarse + jnp.dot(
        jnp.concatenate([target, target], axis=1), parts, preferred_element_type=F32
    )


def solution(mesh):
    return jax.shard_map(
        body,
        mesh=mesh,
        in_specs=(
            P(("row", "col"), None),
            P(("row", "col")),
            P(("row", "col")),
            P(("row", "col")),
            P(("row", "col"), None),
            P(("row", "col")),
            P(("row", "col"), None),
        ),
        out_specs=P(("row", "col"), None),
        check_vma=False,
    )
```

```python
import jax
import jax.numpy as jnp
from jax import lax
from jax.experimental import pallas as pl
from jax.sharding import PartitionSpec as P

BS = 64
PC = 16
NX = 4
NZ = 8
HIGHEST = lax.Precision.HIGHEST
F32 = jnp.float32
BF16 = jnp.bfloat16
F16 = jnp.float16

X_GROUPS = [[x * NZ + z for x in range(NX)] for z in range(NZ)]
Z_GROUPS = [[x * NZ + z for z in range(NZ)] for x in range(NX)]


def spread(values, groups):
    count = len(groups[0])
    copies = jnp.broadcast_to(values[None], (count,) + values.shape)
    moved = lax.all_to_all(copies, "col", 0, 0, axis_index_groups=groups, tiled=True)
    return moved.reshape((count * values.shape[0],) + values.shape[1:])


def shift_x(step):
    return [(x * NZ + z, (x + step) % NX * NZ + z) for x in range(NX) for z in range(NZ)]


def power_of_two(exponent):
    return lax.reduce_precision(jnp.exp2(exponent), 8, 7)


def two_parts(values):
    high = lax.reduce_precision(values, 8, 7)
    return high.astype(BF16), (values - high).astype(BF16)


def select_rows(place, pieces):
    slots = place.shape[0]
    width = pieces[0].shape[1]
    block = 1024

    def kernel(place_ref, *refs):
        out_ref = refs[-1]
        first_row = 0
        total = jnp.zeros(out_ref.shape, F32)
        for ref in refs[:-1]:
            rows = ref.shape[0]
            column = lax.broadcasted_iota(jnp.int32, (slots, rows), 1) + first_row
            chosen = (place_ref[...] == column).astype(F32).astype(BF16)
            total += jnp.dot(chosen, ref[...], preferred_element_type=F32)
            first_row += rows
        out_ref[...] = total.astype(BF16)

    return pl.pallas_call(
        kernel,
        grid=(width // block,),
        in_specs=[pl.BlockSpec((slots, 1), lambda n: (0, 0))]
        + [pl.BlockSpec((piece.shape[0], block), lambda n: (0, n)) for piece in pieces],
        out_specs=pl.BlockSpec((slots, block), lambda n: (0, n)),
        out_shape=jax.ShapeDtypeStruct((slots, width), BF16),
    )(place[:, None], *pieces)


def body(a_blocks, blk_row, blk_col, drop_mask, prolong, agg_label, inv_diag):
    slot_count = a_blocks.shape[0]
    per_device = prolong.shape[0]
    width = prolong.shape[1]
    col_count = lax.axis_size("col")
    row_index = lax.axis_index("row")
    col_index = lax.axis_index("col")
    span = col_count * per_device
    panel_first = row_index * span
    own_first = panel_first + col_index * per_device

    both = spread(jnp.concatenate([prolong, inv_diag], axis=1), Z_GROUPS)

    labelled = jnp.concatenate(
        [prolong, jnp.broadcast_to(agg_label.astype(BF16)[:, None], (per_device, 128))], axis=1
    )
    col_panel = lax.all_gather(labelled, "row", axis=0, tiled=True)

    both, col_panel, blk_row, blk_col, drop_mask, own_label, own_inv = lax.optimization_barrier(
        (both, col_panel, blk_row, blk_col, drop_mask, agg_label, inv_diag)
    )
    row_panel = spread(both[:, :width], X_GROUPS)
    inv_own = both[:, width:]
    half = inv_own.shape[0] // 2
    inv_left = lax.ppermute(inv_own, "col", shift_x(1))
    inv_right = lax.ppermute(inv_own, "col", shift_x(-1))
    inv_far_a = lax.ppermute(inv_left[:half], "col", shift_x(1))
    inv_far_b = lax.ppermute(inv_right[half:], "col", shift_x(-1))

    keep = (drop_mask == 1) | (blk_row == blk_col)
    local_row = blk_row - panel_first
    matrices = a_blocks.reshape(slot_count, BS, BS)

    pick = (local_row[:, None] == jnp.arange(span)[None, :]) & ~keep[:, None]
    row_blocks = jnp.dot(pick.astype(BF16), row_panel, preferred_element_type=F32).astype(BF16)
    drop_terms = jnp.einsum(
        "sij,sjk->sik",
        matrices,
        row_blocks.reshape(slot_count, BS, PC),
        preferred_element_type=F32,
    ).reshape(slot_count, width)
    drop_parts = jnp.concatenate(two_parts(drop_terms), axis=0)
    largest = jnp.max(jnp.abs(drop_terms), axis=1)
    remote = (local_row // per_device != col_index) & ~keep
    place = (jnp.arange(span)[:, None] == local_row[None, :]) & remote[None, :]
    largest = jnp.max(jnp.where(place, largest[None, :], 0.0), axis=1)
    exponent = jnp.floor(jnp.log2(jnp.clip(largest, 1e-30, 1e30)))
    place = jnp.where(place, power_of_two(-exponent)[:, None], 0.0).astype(BF16)
    sums = jnp.dot(jnp.concatenate([place, place], axis=1), drop_parts, preferred_element_type=F32)
    sums = jnp.concatenate(
        [sums.astype(F16), jnp.broadcast_to(exponent.astype(F16)[:, None], (span, 128))], axis=1
    ).reshape(col_count, per_device, width + 128)
    arrived = lax.all_to_all(sums, "col", 0, 0, tiled=True)
    arrived = arrived.reshape(col_count, per_device, width + 128)
    factor = power_of_two(arrived[:, :, width:].astype(F32))[:, :, :1]
    own = (blk_row[None, :] == own_first + jnp.arange(per_device)[:, None]) & ~keep[None, :]
    own = own.astype(BF16)
    lumped = jnp.dot(jnp.concatenate([own, own], axis=1), drop_parts, preferred_element_type=F32)
    lumped = lumped + jnp.sum(arrived[:, :, :width].astype(F32) * factor, axis=0)
    scaled_lumped = jnp.einsum(
        "eij,ejk->eik",
        own_inv.astype(F32).reshape(per_device, BS, BS),
        lumped.reshape(per_device, BS, PC),
        precision=HIGHEST,
    ).reshape(per_device, width)

    col_place = blk_col // span * per_device + blk_col % per_device
    pick = col_place[:, None] == jnp.arange(col_panel.shape[0])[None, :]
    picked = jnp.dot(pick.astype(BF16), col_panel, preferred_element_type=F32)
    col_label = picked[:, width]
    col_blocks = (picked[:, :width] * keep[:, None].astype(F32)).astype(BF16)
    kept_terms = jnp.einsum(
        "sij,sjk->sik",
        matrices,
        col_blocks.reshape(slot_count, BS, PC),
        preferred_element_type=F32,
    ).reshape(slot_count, width)
    col_run = blk_col // per_device
    row_run = blk_row // per_device
    same_group = (
        (blk_row[:, None] == blk_row[None, :])
        & (col_run[:, None] == col_run[None, :])
        & (col_label[:, None] == col_label[None, :])
    ).astype(BF16)
    parts = jnp.concatenate(two_parts(kept_terms), axis=0)
    grouped = jnp.dot(
        jnp.concatenate([same_group, same_group], axis=1), parts, preferred_element_type=F32
    )

    part_rows = NZ * per_device
    distance = (col_index // NZ - local_row // part_rows) % NX
    inverse = select_rows(
        distance * part_rows + local_row % part_rows,
        (inv_own, inv_left, inv_far_a, inv_far_b, inv_right),
    )
    inverse = inverse.reshape(slot_count, BS, BS)
    parts = [part.reshape(slot_count, BS, PC) for part in two_parts(grouped)]
    coarse = jnp.einsum(
        "sij,sjk->sik", inverse, jnp.concatenate(parts, axis=2), preferred_element_type=F32
    )
    coarse = (coarse[:, :, :PC] + coarse[:, :, PC:]).reshape(slot_count, width)

    target = (
        (blk_row[:, None] == own_first + jnp.arange(per_device)[None, :])
        & (col_run == row_run)[:, None]
        & (col_label[:, None] == own_label.astype(F32)[None, :])
    )
    target = target.astype(BF16)
    parts = jnp.concatenate(two_parts(scaled_lumped), axis=0)
    return coarse + jnp.dot(
        jnp.concatenate([target, target], axis=1), parts, preferred_element_type=F32
    )


def solution(mesh):
    return jax.shard_map(
        body,
        mesh=mesh,
        in_specs=(
            P(("row", "col"), None),
            P(("row", "col")),
            P(("row", "col")),
            P(("row", "col")),
            P(("row", "col"), None),
            P(("row", "col")),
            P(("row", "col"), None),
        ),
        out_specs=P(("row", "col"), None),
        check_vma=False,
    )
```

```python
import jax
import jax.numpy as jnp
from jax import lax
from jax.sharding import PartitionSpec as P

BS = 64
PC = 16
NX = 4
NZ = 8
HIGHEST = lax.Precision.HIGHEST
F32 = jnp.float32
BF16 = jnp.bfloat16
F16 = jnp.float16

X_GROUPS = [[x * NZ + z for x in range(NX)] for z in range(NZ)]
Z_GROUPS = [[x * NZ + z for z in range(NZ)] for x in range(NX)]


def spread(values, groups):
    count = len(groups[0])
    copies = jnp.broadcast_to(values[None], (count,) + values.shape)
    moved = lax.all_to_all(copies, "col", 0, 0, axis_index_groups=groups, tiled=True)
    return moved.reshape((count * values.shape[0],) + values.shape[1:])


def shift_x(step):
    return [(x * NZ + z, (x + step) % NX * NZ + z) for x in range(NX) for z in range(NZ)]


def power_of_two(exponent):
    return lax.reduce_precision(jnp.exp2(exponent), 8, 7)


def two_parts(values):
    high = lax.reduce_precision(values, 8, 7)
    return high.astype(BF16), (values - high).astype(BF16)


def body(a_blocks, blk_row, blk_col, drop_mask, prolong, agg_label, inv_diag):
    slot_count = a_blocks.shape[0]
    per_device = prolong.shape[0]
    width = prolong.shape[1]
    col_count = lax.axis_size("col")
    row_index = lax.axis_index("row")
    col_index = lax.axis_index("col")
    span = col_count * per_device
    panel_first = row_index * span
    own_first = panel_first + col_index * per_device

    labelled = jnp.concatenate(
        [prolong, jnp.broadcast_to(agg_label.astype(BF16)[:, None], (per_device, 128))], axis=1
    )
    joined = jnp.concatenate([prolong, inv_diag], axis=1)
    joined, labelled = lax.optimization_barrier((joined, labelled))
    both = spread(joined, Z_GROUPS)

    col_panel = lax.all_gather(labelled, "row", axis=0, tiled=True)

    both, col_panel, a_blocks, blk_row, blk_col, drop_mask, own_label, own_inv = (
        lax.optimization_barrier(
            (both, col_panel, a_blocks, blk_row, blk_col, drop_mask, agg_label, inv_diag)
        )
    )
    row_panel = spread(both[:, :width], X_GROUPS)
    inv_parts = [both[:, width:]]
    for k in (1, 2, 3):
        inv_parts.append(lax.ppermute(inv_parts[0], "col", shift_x(k)))

    keep = (drop_mask == 1) | (blk_row == blk_col)
    local_row = blk_row - panel_first
    matrices = a_blocks.reshape(slot_count, BS, BS)

    pick = (local_row[:, None] == jnp.arange(span)[None, :]) & ~keep[:, None]
    row_blocks = jnp.dot(pick.astype(BF16), row_panel, preferred_element_type=F32).astype(BF16)
    drop_terms = jnp.einsum(
        "sij,sjk->sik",
        matrices,
        row_blocks.reshape(slot_count, BS, PC),
        preferred_element_type=F32,
    ).reshape(slot_count, width)
    drop_parts = jnp.concatenate(two_parts(drop_terms), axis=0)
    largest = jnp.max(jnp.abs(drop_terms), axis=1)
    remote = (local_row // per_device != col_index) & ~keep
    place = (jnp.arange(span)[:, None] == local_row[None, :]) & remote[None, :]
    largest = jnp.max(jnp.where(place, largest[None, :], 0.0), axis=1)
    exponent = jnp.floor(jnp.log2(jnp.clip(largest, 1e-30, 1e30)))
    place = jnp.where(place, power_of_two(-exponent)[:, None], 0.0).astype(BF16)
    sums = jnp.dot(jnp.concatenate([place, place], axis=1), drop_parts, preferred_element_type=F32)
    sums = jnp.concatenate(
        [sums.astype(F16), jnp.broadcast_to(exponent.astype(F16)[:, None], (span, 128))], axis=1
    ).reshape(col_count, per_device, width + 128)
    arrived = lax.all_to_all(sums, "col", 0, 0, tiled=True)
    arrived = arrived.reshape(col_count, per_device, width + 128)
    factor = power_of_two(arrived[:, :, width:].astype(F32))[:, :, :1]
    own = (blk_row[None, :] == own_first + jnp.arange(per_device)[:, None]) & ~keep[None, :]
    own = own.astype(BF16)
    own_lumped = lax.optimization_barrier(
        jnp.dot(jnp.concatenate([own, own], axis=1), drop_parts, preferred_element_type=F32)
    )
    lumped = own_lumped + jnp.sum(arrived[:, :, :width].astype(F32) * factor, axis=0)
    scaled_lumped = jnp.einsum(
        "eij,ejk->eik",
        own_inv.astype(F32).reshape(per_device, BS, BS),
        lumped.reshape(per_device, BS, PC),
        precision=HIGHEST,
    ).reshape(per_device, width)

    col_place = blk_col // span * per_device + blk_col % per_device
    pick = col_place[:, None] == jnp.arange(col_panel.shape[0])[None, :]
    picked = jnp.dot(pick.astype(BF16), col_panel, preferred_element_type=F32)
    col_label = picked[:, width]
    col_blocks = (picked[:, :width] * keep[:, None].astype(F32)).astype(BF16)
    kept_terms = jnp.einsum(
        "sij,sjk->sik",
        matrices,
        col_blocks.reshape(slot_count, BS, PC),
        preferred_element_type=F32,
    ).reshape(slot_count, width)
    col_run = blk_col // per_device
    row_run = blk_row // per_device
    same_group = (
        (blk_row[:, None] == blk_row[None, :])
        & (col_run[:, None] == col_run[None, :])
        & (col_label[:, None] == col_label[None, :])
    ).astype(BF16)
    parts = jnp.concatenate(two_parts(kept_terms), axis=0)
    grouped = jnp.dot(
        jnp.concatenate([same_group, same_group], axis=1), parts, preferred_element_type=F32
    )

    part_rows = NZ * per_device
    row_x = local_row // part_rows
    inverse = None
    for k in range(NX):
        at = jnp.where((col_index // NZ - row_x) % NX == k, local_row % part_rows, -1)
        pick = (at[:, None] == jnp.arange(part_rows)[None, :]).astype(BF16)
        piece = jnp.dot(pick, inv_parts[k], preferred_element_type=F32)
        inverse = piece if inverse is None else inverse + piece
    inverse = inverse.astype(BF16)
    inverse = inverse.reshape(slot_count, BS, BS)
    parts = [part.reshape(slot_count, BS, PC) for part in two_parts(grouped)]
    coarse = jnp.einsum(
        "sij,sjk->sik", inverse, jnp.concatenate(parts, axis=2), preferred_element_type=F32
    )
    coarse = (coarse[:, :, :PC] + coarse[:, :, PC:]).reshape(slot_count, width)

    target = (
        (blk_row[:, None] == own_first + jnp.arange(per_device)[None, :])
        & (col_run == row_run)[:, None]
        & (col_label[:, None] == own_label.astype(F32)[None, :])
    )
    target = target.astype(BF16)
    parts = jnp.concatenate(two_parts(scaled_lumped), axis=0)
    return coarse + jnp.dot(
        jnp.concatenate([target, target], axis=1), parts, preferred_element_type=F32
    )


def solution(mesh):
    return jax.shard_map(
        body,
        mesh=mesh,
        in_specs=(
            P(("row", "col"), None),
            P(("row", "col")),
            P(("row", "col")),
            P(("row", "col")),
            P(("row", "col"), None),
            P(("row", "col")),
            P(("row", "col"), None),
        ),
        out_specs=P(("row", "col"), None),
        check_vma=False,
    )
```
